32 devices in a mesh: rep: 4 (over y, x), fsdp: 8 (over z, core).
Axes of the slice: x: 2, y: 2, z: 4, core: 2. Of those that a mesh axis runs over, the one named last changes fastest.
Arguments:
- patches: float32 [8192, 1152], P(('rep', 'fsdp')), may hold values from -6 to 6
- cotangent: float32 [8192, 1152], P(('rep', 'fsdp')), may hold values from -6 to 6
- image_ids: int32 [4, 2048], P('rep'), may hold values from 0 to 4, never falling along the last dimension, each value on 1 to 729 neighbouring positions
- input_weight: bfloat16 [2, 1152, 3456], P(None, 'fsdp'), as said below
- output_weight: bfloat16 [2, 1152, 1152], P(None, 'fsdp'), may hold values from -1 to 1
- expand_weight: bfloat16 [2, 1152, 4304], P(None, 'fsdp'), may hold values from -0.1875 to 0.1875
- reduce_weight: bfloat16 [2, 4304, 1152], P(None, 'fsdp'), may hold values from -0.09375 to 0.09375
- first_gain: bfloat16 [2, 1152], P(None, 'fsdp'), may hold values from 0.099609375 to 1.8984375
- first_shift: bfloat16 [2, 1152], P(None, 'fsdp'), may hold values from -3 to 3
- query_bias: bfloat16 [2, 1152], P(None, 'fsdp'), may hold values from -3 to 3
- value_bias: bfloat16 [2, 1152], P(None, 'fsdp'), may hold values from -3 to 3
- output_bias: bfloat16 [2, 1152], P(None, 'fsdp'), may hold values from -3 to 3
- second_gain: bfloat16 [2, 1152], P(None, 'fsdp'), may hold values from 0.099609375 to 1.8984375
- second_shift: bfloat16 [2, 1152], P(None, 'fsdp'), may hold values from -3 to 3
- expand_bias: bfloat16 [2, 4304], P(None, 'fsdp'), may hold values from -3 to 3
- reduce_bias: bfloat16 [2, 1152], P(None, 'fsdp'), may hold values from -3 to 3
Outputs:
- encoded: float32 [8192, 1152], P(('rep', 'fsdp'))
- patch_grad: float32 [8192, 1152], P(('rep', 'fsdp'))
- grad_input_weight: float32 [2, 1152, 3456], P(None, 'fsdp')
- grad_output_weight: float32 [2, 1152, 1152], P(None, 'fsdp')
- grad_expand_weight: float32 [2, 1152, 4304], P(None, 'fsdp')
- grad_reduce_weight: float32 [2, 4304, 1152], P(None, 'fsdp')
- grad_first_gain: float32 [2, 1152], P(None, 'fsdp')
- grad_first_shift: float32 [2, 1152], P(None, 'fsdp')
- grad_query_bias: float32 [2, 1152], P(None, 'fsdp')
- grad_value_bias: float32 [2, 1152], P(None, 'fsdp')
- grad_output_bias: float32 [2, 1152], P(None, 'fsdp')
- grad_second_gain: float32 [2, 1152], P(None, 'fsdp')
- grad_second_shift: float32 [2, 1152], P(None, 'fsdp')
- grad_expand_bias: float32 [2, 4304], P(None, 'fsdp')
- grad_reduce_bias: float32 [2, 1152], P(None, 'fsdp')
The draws below stay inside these ranges and needn't reach their ends.
Inputs may be any that keep to these rules, and one draw needn't show every extreme that they name: `image_ids`: within each row, one group's 2048 tokens in order, ids never fall and each image holds 1 to 729 consecutive tokens; some image holds exactly 729. `input_weight`: projection weights of fan-in 1152.
All inputs are finite; a program needn't handle non-finite values.
Results may differ from the reference program's by a relative error of at most 0.014.
The reference program's roundings to bfloat16 on the way count: a program that leaves them out, or rounds other values in their place, can miss the bound.
Values may be sent and summed in bfloat16 or wider, within the bound.
No kernel may reach another device: no remote copies, remote signals or barrier semaphores. Data moves between devices by JAX's collectives and lax.ppermute only.
A program may use at most 384 MiB of HBM per device.

```python
import math
from functools import partial
import jax
import jax.numpy as jnp
import numpy as np
from jax import lax

D = 1152
FF = 4304
HEADS = 16
HEAD_DIM = 72
MOST = 729
LAYERS = 2
GROUP_TOK = 2048
TOKENS = 8192
IMG_GRP = 5
N_REP = 4


def draw_input_weight(key, part):
    value_key = jax.random.fold_in(key, 101)
    head_key = jax.random.fold_in(key, 202)
    shape = (LAYERS, D, 3 * D)
    values = jax.random.truncated_normal(value_key, -4.0, 4.0, shape, jnp.float32)
    chosen = jax.random.randint(head_key, (LAYERS, 1, 1), 0, HEADS)
    column = lax.broadcasted_iota(jnp.int32, (LAYERS, 1, 3 * D), 2)
    head_of = column % D // HEAD_DIM
    boost = jnp.where((head_of == chosen) & (column < 2 * D), 2.0, 1.0)
    return (values * boost * (1.0 / math.sqrt(D))).astype(jnp.bfloat16)


def levels(key, dims, pieces, least, high):
    def one(axis_at, shards_of):
        heights = jax.random.uniform(jax.random.fold_in(jax.random.fold_in(key, 6), axis_at), (shards_of,), jnp.float32, least / len(pieces), high / len(pieces))
        return jnp.repeat(jnp.exp(heights), dims[axis_at] // shards_of).reshape((-1,) + (1,) * (len(dims) - axis_at - 1))

    level = one(*pieces[0])
    for cut in pieces[1:]:
        level = level * one(*cut)
    return level


def profile(count, total, reach, slope):
    portions = [(1 << 20) // math.isqrt(rank ** slope) + 1 for rank in range(2, count + 1)]
    rest, given = total - reach - (count - 1), [1] * (count - 1)
    while rest > 0:
        free = [i for i in range(count - 1) if given[i] < reach]
        pool, budget = sum([portions[i] for i in free]), rest
        for i in free:
            more = min(reach - given[i], max(1, budget * portions[i] // pool), rest)
            given[i] = given[i] + more
            rest = rest - more
    return np.array([reach] + given)


def uneven_parts(key, count, total, most, slope):
    if count == 2:
        one = jax.random.randint(key, (), max(1, total - most), min(most, total - 1) + 1)
        return jnp.stack([one, total - one])
    lengths = jnp.asarray(profile(count, total, most, slope), jnp.int32)
    twos = (count - 1) // 2
    donor, taker = lengths[1:1 + 2 * twos:2], lengths[2:2 + 2 * twos:2]
    room = jnp.minimum(donor - 1, most - taker)
    moved = jax.random.randint(jax.random.fold_in(key, 1), (twos,), 0, 1 << 20) % (room + 1)
    lengths = lengths.at[1:1 + 2 * twos:2].set(donor - moved).at[2:2 + 2 * twos:2].set(taker + moved)
    return lengths[jax.random.permutation(jax.random.fold_in(key, 2), count)]


def noise(stream_key, dims, deviation, bound, cuts=(), dtype=jnp.bfloat16):
    level = levels(stream_key, dims, cuts, -0.22, 0.18) if cuts else 1.0
    values = jax.random.normal(stream_key, dims, jnp.float32) * deviation * level
    return jnp.minimum(jnp.maximum(values, -bound), bound).astype(dtype)


def setup_inputs(seed: int = 0) -> dict:
    keys = jax.random.split(jax.random.key(seed), 17)
    return {
        "patches": noise(keys[0], (TOKENS, D), 1.0, 6.0, ((0, 32),), jnp.float32),
        "cotangent": noise(keys[1], (TOKENS, D), 1.0, 6.0, ((0, 32),), jnp.float32),
        "image_ids": jax.vmap(lambda own: jnp.searchsorted(jnp.cumsum(uneven_parts(own, IMG_GRP, GROUP_TOK, MOST, 1)), jnp.arange(GROUP_TOK), side="right"))(jax.random.split(keys[2], N_REP)).reshape((N_REP, GROUP_TOK)).astype(jnp.int32),
        "input_weight": draw_input_weight(jax.random.fold_in(keys[16], 71), 0),
        "output_weight": noise(keys[4], (LAYERS, D, D), (max(D // 32, 1)) ** -0.5, 1.0, ((1, 8),)),
        "expand_weight": noise(keys[5], (LAYERS, D, FF), D ** -0.5, 0.1875, ((1, 8),)),
        "reduce_weight": noise(keys[6], (LAYERS, FF, D), FF ** -0.5, 0.09375, ((1, 8),)),
        "first_gain": jnp.clip(1.0 + 0.18 * jax.random.normal(keys[7], (LAYERS, D), jnp.float32), 0.099609375, 1.8984375).astype(jnp.bfloat16),
        "first_shift": noise(keys[8], (LAYERS, D), 0.5, 3.0, ((1, 8),)),
        "query_bias": noise(keys[9], (LAYERS, D), 0.5, 3.0, ((1, 8),)),
        "value_bias": noise(keys[10], (LAYERS, D), 0.5, 3.0, ((1, 8),)),
        "output_bias": noise(keys[11], (LAYERS, D), 0.5, 3.0, ((1, 8),)),
        "second_gain": jnp.clip(1.0 + 0.18 * jax.random.normal(keys[12], (LAYERS, D), jnp.float32), 0.099609375, 1.8984375).astype(jnp.bfloat16),
        "second_shift": noise(keys[13], (LAYERS, D), 0.5, 3.0, ((1, 8),)),
        "expand_bias": noise(keys[14], (LAYERS, FF), 0.5, 3.0, ((1, 8),)),
        "reduce_bias": noise(keys[15], (LAYERS, D), 0.5, 3.0, ((1, 8),)),
    }


EPSILON = 1e-06
GELU_COEF = math.sqrt(2.0 / math.pi)
MASKED = -1e+30

def norm_forward(values, norm_gain, norm_bias):
    centre = lax.optimization_barrier(jnp.mean(values, axis=-1, keepdims=True))
    shifted = values - centre
    spread = lax.optimization_barrier(jnp.mean(shifted * shifted, axis=-1, keepdims=True))
    inverse = lax.rsqrt(spread + EPSILON)
    scaled = shifted * inverse
    return (scaled * norm_gain + norm_bias, scaled, inverse)

def norm_backward(upstream, scaled, inverse, norm_gain):
    weighted = upstream * norm_gain
    mean_one = lax.optimization_barrier(jnp.mean(weighted, axis=-1, keepdims=True))
    mean_two = lax.optimization_barrier(jnp.mean(weighted * scaled, axis=-1, keepdims=True))
    result = inverse * (weighted - mean_one - scaled * mean_two)
    return (result, lax.optimization_barrier(jnp.sum(upstream * scaled, axis=0)), lax.optimization_barrier(jnp.sum(upstream, axis=0)))

def gelu_tanh(inputs):
    inside = GELU_COEF * (inputs + 0.044715 * inputs * inputs * inputs)
    return 0.5 * inputs * (1.0 + jnp.tanh(inside))

def gelu_slope(inputs):
    inside = GELU_COEF * (inputs + 0.044715 * inputs * inputs * inputs)
    tangent = jnp.tanh(inside)
    return 0.5 * (1.0 + tangent) + 0.5 * inputs * (1.0 - tangent * tangent) * GELU_COEF * (1.0 + 3.0 * 0.044715 * inputs * inputs)

def dot_first(left_op, right_op):
    return lax.dot_general(left_op, right_op, (((0,), (0,)), ((), ())), preferred_element_type=jnp.float32)

def dot_last(left_op, right_op):
    return lax.dot_general(left_op, right_op, (((1,), (1,)), ((), ())), preferred_element_type=jnp.float32)

def split_heads(matrix):
    return jnp.transpose(matrix.reshape(matrix.shape[0], HEADS, HEAD_DIM), (1, 0, 2))

def join_heads(stacked):
    return jnp.transpose(stacked, (1, 0, 2)).reshape(stacked.shape[1], HEADS * HEAD_DIM)

def head_scores(query_head, key_head, key_mask):
    scores = dot_last(query_head, key_head) * (1.0 / math.sqrt(HEAD_DIM))
    return jnp.where(key_mask, scores, MASKED)

def head_forward(operands, key_mask):
    query_head, key_head, value_head = operands
    scores = head_scores(query_head, key_head, key_mask)
    highest = lax.optimization_barrier(jnp.max(scores, axis=-1, keepdims=True))
    log_sum = highest + jnp.log(lax.optimization_barrier(jnp.sum(jnp.exp(scores - highest), axis=-1, keepdims=True)))
    weights_low = jnp.exp(scores - log_sum).astype(jnp.bfloat16)
    return (jnp.dot(weights_low, value_head, preferred_element_type=jnp.float32), log_sum[:, 0])

def head_backward(operands, key_mask):
    query_head, key_head, value_head, grad_head, attended_head, log_sum = operands
    scores = head_scores(query_head, key_head, key_mask)
    probabilities = jnp.exp(scores - log_sum[:, None])
    grad_probs = dot_last(grad_head, value_head)
    row_dot = lax.optimization_barrier(jnp.sum(grad_head.astype(jnp.float32) * attended_head, axis=-1, keepdims=True))
    grad_scores = (probabilities * (grad_probs - row_dot) * (1.0 / math.sqrt(HEAD_DIM))).astype(jnp.bfloat16)
    grad_query = jnp.dot(grad_scores, key_head, preferred_element_type=jnp.float32)
    grad_keys = dot_first(grad_scores, query_head)
    grad_values = dot_first(probabilities.astype(jnp.bfloat16), grad_head)
    return (grad_query, grad_keys, grad_values)

def layer_forward(stream, key_mask, params):
    input_matrix, output_matrix, expand_matrix, reduce_matrix, gain_one, shift_one, bias_query, bias_value, bias_output, gain_two, shift_two, bias_expand, bias_reduce = params
    normed, scaled_one, inverse_one = norm_forward(stream, gain_one.astype(jnp.float32), shift_one.astype(jnp.float32))
    normed_low = normed.astype(jnp.bfloat16)
    projected = jnp.dot(normed_low, input_matrix, preferred_element_type=jnp.float32)
    queries = (projected[:, :D] + bias_query.astype(jnp.float32)).astype(jnp.bfloat16)
    key_rows = projected[:, D:2 * D].astype(jnp.bfloat16)
    value_rows = (projected[:, 2 * D:] + bias_value.astype(jnp.float32)).astype(jnp.bfloat16)
    head_out, log_sums = lax.map(partial(head_forward, key_mask=key_mask), (split_heads(queries), split_heads(key_rows), split_heads(value_rows)))
    attended = join_heads(head_out)
    attended_low = attended.astype(jnp.bfloat16)
    middle = stream + jnp.dot(attended_low, output_matrix, preferred_element_type=jnp.float32) + bias_output.astype(jnp.float32)
    normed_two, scaled_two, inverse_two = norm_forward(middle, gain_two.astype(jnp.float32), shift_two.astype(jnp.float32))
    normed_two = normed_two.astype(jnp.bfloat16)
    hidden_pre = jnp.dot(normed_two, expand_matrix, preferred_element_type=jnp.float32) + bias_expand.astype(jnp.float32)
    hidden_low = gelu_tanh(hidden_pre).astype(jnp.bfloat16)
    output = middle + jnp.dot(hidden_low, reduce_matrix, preferred_element_type=jnp.float32) + bias_reduce.astype(jnp.float32)
    stored = (scaled_one, inverse_one, normed_low, queries, key_rows, value_rows, attended, log_sums, attended_low, scaled_two, inverse_two, normed_two, hidden_pre, hidden_low)
    return (output, stored)

def layer_backward(upstream, key_mask, params, stored):
    input_matrix, output_matrix, expand_matrix, reduce_matrix, gain_one, shift_one, bias_query, bias_value, bias_output, gain_two, shift_two, bias_expand, bias_reduce = params
    scaled_one, inverse_one, normed_low, queries, key_rows, value_rows, attended, log_sums, attended_low, scaled_two, inverse_two, normed_two, hidden_pre, hidden_low = stored
    upstream_low = upstream.astype(jnp.bfloat16)
    grad_reduce = dot_first(hidden_low, upstream_low)
    grad_reduce_bias = lax.optimization_barrier(jnp.sum(upstream, axis=0))
    grad_pre = dot_last(upstream_low, reduce_matrix) * gelu_slope(hidden_pre)
    grad_pre_low = grad_pre.astype(jnp.bfloat16)
    grad_expand = dot_first(normed_two, grad_pre_low)
    grad_expand_bias = lax.optimization_barrier(jnp.sum(grad_pre, axis=0))
    grad_normed_two = dot_last(grad_pre_low, expand_matrix)
    part_two, grad_gain_two, grad_shift_two = norm_backward(grad_normed_two, scaled_two, inverse_two, gain_two.astype(jnp.float32))
    grad_middle = upstream + part_two
    grad_middle_low = grad_middle.astype(jnp.bfloat16)
    grad_output = dot_first(attended_low, grad_middle_low)
    grad_output_bias = lax.optimization_barrier(jnp.sum(grad_middle, axis=0))
    grad_attended = dot_last(grad_middle_low, output_matrix).astype(jnp.bfloat16)
    grad_query_heads, grad_key_heads, grad_value_heads = lax.map(partial(head_backward, key_mask=key_mask), (split_heads(queries), split_heads(key_rows), split_heads(value_rows), split_heads(grad_attended), split_heads(attended), log_sums))
    grad_queries = join_heads(grad_query_heads)
    grad_keys = join_heads(grad_key_heads)
    grad_values = join_heads(grad_value_heads)
    grad_projected = jnp.concatenate([grad_queries, grad_keys, grad_values], axis=1).astype(jnp.bfloat16)
    grad_input = dot_first(normed_low, grad_projected)
    grad_query_bias = lax.optimization_barrier(jnp.sum(grad_queries, axis=0))
    grad_value_bias = lax.optimization_barrier(jnp.sum(grad_values, axis=0))
    grad_normed = dot_last(grad_projected, input_matrix)
    part_one, grad_gain_one, grad_shift_one = norm_backward(grad_normed, scaled_one, inverse_one, gain_one.astype(jnp.float32))
    downstream = grad_middle + part_one
    grads = (grad_input, grad_output, grad_expand, grad_reduce, grad_gain_one, grad_shift_one, grad_query_bias, grad_value_bias, grad_output_bias, grad_gain_two, grad_shift_two, grad_expand_bias, grad_reduce_bias)
    return (downstream, grads)

def reference(patches, cotangent, image_ids, input_weight, output_weight, expand_weight, reduce_weight, first_gain, first_shift, query_bias, value_bias, output_bias, second_gain, second_shift, expand_bias, reduce_bias):

    def layer_params(layer_index):
        return (input_weight[layer_index], output_weight[layer_index], expand_weight[layer_index], reduce_weight[layer_index], first_gain[layer_index], first_shift[layer_index], query_bias[layer_index], value_bias[layer_index], output_bias[layer_index], second_gain[layer_index], second_shift[layer_index], expand_bias[layer_index], reduce_bias[layer_index])
    encoded_parts = []
    gradient_parts = []
    totals = None
    for group_index in range(N_REP):
        stream = patches[group_index * GROUP_TOK:(group_index + 1) * GROUP_TOK]
        ids_row = image_ids[group_index]
        key_mask = ids_row[:, None] == ids_row[None, :]
        stored_all = []
        for layer_index in range(LAYERS):
            stream, stored = layer_forward(stream, key_mask, layer_params(layer_index))
            stored_all.append(stored)
        encoded_parts.append(stream)
        upstream = cotangent[group_index * GROUP_TOK:(group_index + 1) * GROUP_TOK]
        layer_grads = [None] * LAYERS
        for layer_index in range(LAYERS - 1, -1, -1):
            upstream, grads = layer_backward(upstream, key_mask, layer_params(layer_index), stored_all[layer_index])
            layer_grads[layer_index] = grads
        gradient_parts.append(upstream)
        stacked = tuple((jnp.stack([layer_grads[layer_index][member] for layer_index in range(LAYERS)]) for member in range(13)))
        if totals is None:
            totals = stacked
        else:
            totals = tuple((earlier + later for earlier, later in zip(totals, stacked)))
    encoded = jnp.concatenate(encoded_parts, axis=0)
    patch_grad = jnp.concatenate(gradient_parts, axis=0)
    return (encoded, patch_grad, totals[0], totals[1], totals[2], totals[3], totals[4], totals[5], totals[6], totals[7], totals[8], totals[9], totals[10], totals[11], totals[12])
```

```python
import functools
import math

import jax
import jax.numpy as jnp
from jax import lax
from jax.experimental import pallas as pl
from jax.experimental.pallas import tpu as pltpu
from jax.sharding import Mesh
from jax.sharding import PartitionSpec as P

HEADS = 16
CORES = 2
LANES = 128
EPSILON = 1e-06
GELU_COEF = math.sqrt(2.0 / math.pi)
MASKED = -1e30
F32 = jnp.float32
BF16 = jnp.bfloat16


def up(n, to=LANES):
    return -(-n // to) * to


def norm_forward(values, norm_gain, norm_bias):
    centre = jnp.mean(values, axis=-1, keepdims=True)
    shifted = values - centre
    spread = jnp.mean(shifted * shifted, axis=-1, keepdims=True)
    inverse = lax.rsqrt(spread + EPSILON)
    scaled = shifted * inverse
    return (scaled * norm_gain + norm_bias, scaled, inverse)


def norm_backward(upstream, scaled, inverse, norm_gain):
    weighted = upstream * norm_gain
    mean_one = jnp.mean(weighted, axis=-1, keepdims=True)
    mean_two = jnp.mean(weighted * scaled, axis=-1, keepdims=True)
    result = inverse * (weighted - mean_one - scaled * mean_two)
    return (result, jnp.sum(upstream * scaled, axis=0), jnp.sum(upstream, axis=0))


def gelu_tanh(inputs):
    inside = GELU_COEF * (inputs + 0.044715 * inputs * inputs * inputs)
    return 0.5 * inputs * (1.0 + jnp.tanh(inside))


def gelu_slope(inputs):
    inside = GELU_COEF * (inputs + 0.044715 * inputs * inputs * inputs)
    tangent = jnp.tanh(inside)
    return 0.5 * (1.0 + tangent) + 0.5 * inputs * (1.0 - tangent * tangent) * GELU_COEF * (
        1.0 + 3.0 * 0.044715 * inputs * inputs
    )


def dot(left_op, right_op):
    return jnp.dot(left_op, right_op, preferred_element_type=F32)


def dot_first(left_op, right_op):
    return lax.dot_general(
        left_op, right_op, (((0,), (0,)), ((), ())), preferred_element_type=F32
    )


def dot_last(left_op, right_op):
    return lax.dot_general(
        left_op, right_op, (((1,), (1,)), ((), ())), preferred_element_type=F32
    )


def attend_kernel(heads, scale, counts, pairs, q_ref, k_ref, v_ref, qid_ref, kid_ref,
                  out_ref, low_ref, log_ref, high, total, acc):
    here = pl.program_id(0)
    span = q_ref.shape[0]
    high[...] = jnp.full_like(high, MASKED)
    total[...] = jnp.zeros_like(total)
    acc[...] = jnp.zeros_like(acc)

    def step(n, carry):
        there = pairs[here, n]
        rows = pl.ds(pl.multiple_of(there * span, span), span)
        allowed = kid_ref[rows, :] == qid_ref[0]
        for h in range(heads):
            lanes = slice(h * LANES, (h + 1) * LANES)
            scores = dot_last(k_ref[rows, lanes], q_ref[:, lanes]) * scale
            scores = jnp.where(allowed, scores, MASKED)
            old = high[h]
            new = jnp.maximum(old, jnp.max(scores, axis=0, keepdims=True))
            kept = jnp.exp(old - new)
            weights = jnp.exp(scores - new)
            high[h] = new
            total[h] = total[h] * kept + jnp.sum(weights, axis=0, keepdims=True)
            acc[h] = acc[h] * kept + dot_first(v_ref[rows, lanes], weights.astype(BF16))
        return carry

    lax.fori_loop(0, counts[here], step, 0)
    for h in range(heads):
        lanes = slice(h * LANES, (h + 1) * LANES)
        result = (acc[h] / total[h]).T
        out_ref[:, lanes] = result
        low_ref[:, lanes] = result.astype(BF16)
        log_ref[0, h : h + 1, :] = high[h] + jnp.log(total[h])


def attend(projected, ids_column, ids_rows, counts, pairs, heads, scale):
    tokens = projected.shape[0]
    spans, span = ids_rows.shape[0], ids_rows.shape[2]
    wide = heads * LANES
    return pl.pallas_call(
        functools.partial(attend_kernel, heads, scale),
        grid_spec=pltpu.PrefetchScalarGridSpec(
            num_scalar_prefetch=2,
            grid=(spans,),
            in_specs=[
                pl.BlockSpec((span, wide), lambda i, *_: (i, 0)),
                pl.BlockSpec((tokens, wide), lambda i, *_: (0, 1)),
                pl.BlockSpec((tokens, wide), lambda i, *_: (0, 2)),
                pl.BlockSpec((1, 1, span), lambda i, *_: (i, 0, 0)),
                pl.BlockSpec((tokens, 1), lambda i, *_: (0, 0)),
            ],
            out_specs=[
                pl.BlockSpec((span, wide), lambda i, *_: (i, 0)),
                pl.BlockSpec((span, wide), lambda i, *_: (i, 0)),
                pl.BlockSpec((1, heads, span), lambda i, *_: (i, 0, 0)),
            ],
            scratch_shapes=[
                pltpu.VMEM((heads, 1, span), F32),
                pltpu.VMEM((heads, 1, span), F32),
                pltpu.VMEM((heads, LANES, span), F32),
            ],
        ),
        out_shape=[
            jax.ShapeDtypeStruct((tokens, wide), F32),
            jax.ShapeDtypeStruct((tokens, wide), BF16),
            jax.ShapeDtypeStruct((spans, heads, span), F32),
        ],
        cost_estimate=pl.CostEstimate(
            flops=2 * tokens * tokens * wide, bytes_accessed=12 * tokens * wide,
            transcendentals=tokens * tokens * heads // 2),
        name="attend",
    )(counts, pairs, projected, projected, projected, ids_rows, ids_column)


def attend_back_kernel(heads, scale, counts, pairs, q_ref, k_ref, v_ref, up_ref, out_ref, kid_ref,
                       qid_ref, log_ref, grad_ref, sums_ref, grad_q, grad_k, grad_v, dots):
    here = pl.program_id(0)
    span = k_ref.shape[0]
    wide = heads * LANES

    @pl.when(here == 0)
    def _():
        grad_q[...] = jnp.zeros_like(grad_q)
        sums_ref[...] = jnp.zeros_like(sums_ref)
        for i in range(dots.shape[0]):
            rows = slice(i * span, (i + 1) * span)
            for h in range(heads):
                lanes = slice(h * LANES, (h + 1) * LANES)
                product = up_ref[rows, lanes].astype(F32) * out_ref[rows, lanes]
                dots[i, h : h + 1, :] = jnp.sum(product.T, axis=0, keepdims=True)

    grad_k[...] = jnp.zeros_like(grad_k)
    grad_v[...] = jnp.zeros_like(grad_v)

    def step(n, carry):
        there = pairs[here, n]
        rows = pl.ds(pl.multiple_of(there * span, span), span)
        allowed = kid_ref[...] == qid_ref[there]
        for h in range(heads):
            lanes = slice(h * LANES, (h + 1) * LANES)
            queries = q_ref[rows, lanes]
            upstream = up_ref[rows, lanes]
            scores = dot_last(k_ref[:, lanes], queries) * scale
            scores = jnp.where(allowed, scores - log_ref[there, h : h + 1, :], MASKED)
            weights = jnp.exp(scores)
            slope = dot_last(v_ref[:, lanes], upstream) - dots[there, h : h + 1, :]
            slope = (weights * slope * scale).astype(BF16)
            grad_v[:, lanes] += dot(weights.astype(BF16), upstream)
            grad_k[:, lanes] += dot(slope, queries)
            grad_q[rows, lanes] += dot_first(slope, k_ref[:, lanes])
        return carry

    lax.fori_loop(0, counts[here], step, 0)
    mine = pl.ds(pl.multiple_of(here * span, span), span)
    grad_ref[mine, wide : 2 * wide] = grad_k[...].astype(BF16)
    grad_ref[mine, 2 * wide :] = grad_v[...].astype(BF16)
    sums_ref[1:2, :] += jnp.sum(grad_v[...], axis=0, keepdims=True)

    @pl.when(here == pl.num_programs(0) - 1)
    def _():
        grad_ref[:, :wide] = grad_q[...].astype(BF16)
        sums_ref[0:1, :] = jnp.sum(grad_q[...], axis=0, keepdims=True)


def attend_back(projected, upstream, attended, ids_column, ids_rows, log_rows, counts, pairs,
                heads, scale):
    tokens = projected.shape[0]
    spans, span = ids_rows.shape[0], ids_rows.shape[2]
    wide = heads * LANES
    return pl.pallas_call(
        functools.partial(attend_back_kernel, heads, scale),
        grid_spec=pltpu.PrefetchScalarGridSpec(
            num_scalar_prefetch=2,
            grid=(spans,),
            in_specs=[
                pl.BlockSpec((tokens, wide), lambda i, *_: (0, 0)),
                pl.BlockSpec((span, wide), lambda i, *_: (i, 1)),
                pl.BlockSpec((span, wide), lambda i, *_: (i, 2)),
                pl.BlockSpec((tokens, wide), lambda i, *_: (0, 0)),
                pl.BlockSpec((tokens, wide), lambda i, *_: (0, 0)),
                pl.BlockSpec((span, 1), lambda i, *_: (i, 0)),
                pl.BlockSpec((spans, 1, span), lambda i, *_: (0, 0, 0)),
                pl.BlockSpec((spans, heads, span), lambda i, *_: (0, 0, 0)),
            ],
            out_specs=[
                pl.BlockSpec((tokens, 3 * wide), lambda i, *_: (0, 0)),
                pl.BlockSpec((2, wide), lambda i, *_: (0, 0)),
            ],
            scratch_shapes=[
                pltpu.VMEM((tokens, wide), F32),
                pltpu.VMEM((span, wide), F32),
                pltpu.VMEM((span, wide), F32),
                pltpu.VMEM((spans, heads, span), F32),
            ],
        ),
        out_shape=[
            jax.ShapeDtypeStruct((tokens, 3 * wide), BF16),
            jax.ShapeDtypeStruct((2, wide), F32),
        ],
        cost_estimate=pl.CostEstimate(
            flops=5 * tokens * tokens * wide, bytes_accessed=16 * tokens * wide,
            transcendentals=tokens * tokens * heads // 2),
        name="attend_back",
    )(counts, pairs, projected, projected, projected, upstream, attended, ids_column,
      ids_rows, log_rows)


def body(
    reps,
    patches,
    cotangent,
    image_ids,
    input_weight,
    output_weight,
    expand_weight,
    reduce_weight,
    first_gain,
    first_shift,
    query_bias,
    value_bias,
    output_bias,
    second_gain,
    second_shift,
    expand_bias,
    reduce_bias,
):
    layers, own, _ = input_weight.shape
    span, width = patches.shape
    shards = reps * CORES
    tokens = span * shards
    own_ff = reduce_weight.shape[1]
    wide_ff = up(own_ff)
    heads = HEADS // shards
    head_dim = width // HEADS
    scale = 1.0 / math.sqrt(head_dim)
    wide = heads * LANES
    bits = reps.bit_length() - 1
    rep = lax.axis_index("rep")
    line = lax.axis_index("line")
    core = lax.axis_index("core")
    rank = rep * CORES + core
    every = ("rep", "line", "core")

    def ranked(r, z, c):
        return (r * reps + z) * CORES + c

    places = [(r, z, c) for r in range(reps) for z in range(reps) for c in range(CORES)]
    turned = [(ranked(r, z, c), ranked(r ^ z, r, c)) for r, z, c in places]
    turned_back = [(there, here) for here, there in turned]
    mates = [(ranked(r, z, c), ranked(r, z, 1 - c)) for r, z, c in places]

    def flip(step, c):
        return 1 << (step if c == 0 else bits - 1 - step)

    hops = [
        [(ranked(r, z, c), ranked(r ^ flip(step, c), z, c)) for r, z, c in places]
        for step in range(bits)
    ]

    line_hops = [
        [(ranked(r, z, c), ranked(r, z ^ (1 << step), c)) for r, z, c in places]
        for step in range(bits)
    ]
    rep_hops = [
        [(ranked(r, z, c), ranked(r ^ (1 << step), z, c)) for r, z, c in places]
        for step in range(bits)
    ]

    def relocate(array):
        return lax.ppermute(array, every, turned)

    def put_back(array):
        return lax.ppermute(array, every, turned_back)

    def swap(array):
        return lax.ppermute(array, every, mates)

    def after(array, other):
        return array + (other[(0,) * other.ndim] * 0).astype(array.dtype)

    def gather(array):
        for step in range(bits):
            array = jnp.concatenate([array, lax.ppermute(array, every, hops[step])])
        return array, swap(array)

    def scatter(pair, multiply):
        got = swap(multiply(pair[1]).astype(BF16))
        held = multiply(pair[0]) + got.astype(F32)
        for step in range(bits - 1, -1, -1):
            half = held.shape[0] // 2
            got = lax.ppermute(held[half:].astype(BF16), every, hops[step])
            held = held[:half] + got.astype(F32)
        return held

    def mirrored(j):
        return sum(((j >> b) & 1) << (bits - 1 - b) for b in range(bits))

    def spans_of(c):
        return [(jnp.where(c == 0, rep ^ j, rep ^ mirrored(j)) ^ line) * CORES + c
                for j in range(reps)]

    def collect(block, twist):
        block = block[None]
        for step in range(bits):
            block = jnp.concatenate([block, lax.ppermute(block, every, hops[step])])
        parts = []
        for a in range(reps):
            wanted = a ^ rep ^ twist
            part = block[0]
            for j in range(1, reps):
                at = jnp.where(core == 0, j, mirrored(j))
                part = jnp.where(wanted == at, block[j], part)
            parts.append(part)
        return parts

    order = jnp.stack(spans_of(core) + spans_of(1 - core))

    small = jnp.concatenate(
        [first_gain, first_shift, query_bias, value_bias, output_bias, second_gain,
         second_shift, reduce_bias, expand_bias], axis=1)
    small = lax.all_gather(small, ("line", "core"), axis=0, tiled=False)
    mine = lax.dynamic_index_in_dim(small, rank, 0, keepdims=False)
    normed = norm_forward(
        patches, small[:, 0, :own].reshape(width).astype(F32),
        small[:, 0, own : 2 * own].reshape(width).astype(F32))[0]
    normed = relocate(normed.astype(BF16))
    stream = relocate(after(patches, normed))
    ids = relocate(image_ids + (small[0, 0, 0] * 0).astype(jnp.int32))[0]
    ids = jnp.take(ids.reshape(shards, span), order, axis=0)
    ids_rows = ids.reshape(shards, 1, span)
    ids_column = ids.reshape(tokens, 1)
    first, last = ids[:, 0], ids[:, -1]
    meets = (first[:, None] <= last[None, :]) & (first[None, :] <= last[:, None])
    counts = jnp.sum(meets, axis=1, dtype=jnp.int32)
    before = jnp.arange(shards)[:, None] < jnp.arange(shards)[None, :]
    place = jnp.sum(meets[:, :, None] & before[None], axis=1, dtype=jnp.int32)
    chosen = meets[:, :, None] & (place[:, :, None] == jnp.arange(shards))
    pairs = jnp.sum(
        jnp.where(chosen, jnp.arange(shards, dtype=jnp.int32)[None, :, None], 0), axis=1,
        dtype=jnp.int32)

    def whole(index, layer):
        return small[:, layer, index * own : (index + 1) * own].reshape(width).astype(F32)

    def my_part(index, layer):
        return mine[layer, index * own : (index + 1) * own].astype(F32)

    def pad_heads(array):
        array = array.reshape(array.shape[:-1] + (heads, head_dim))
        array = jnp.pad(array, [(0, 0)] * (array.ndim - 1) + [(0, LANES - head_dim)])
        return array.reshape(array.shape[:-2] + (wide,))

    def cut_heads(array):
        array = array.reshape(array.shape[:-1] + (heads, LANES))[..., :head_dim]
        return array.reshape(array.shape[:-2] + (heads * head_dim,))

    start_ff = up(3 * own)

    own_up, own_ff_up = up(own, 16 * reps), up(own_ff, 16 * reps)

    def fetch_columns(of, other):
        kept, got = after(of(core), other), swap(after(of(1 - core), other))
        rows = jnp.where(core == 0, jnp.stack([kept, got]), jnp.stack([got, kept]))
        return lax.all_gather(rows.reshape(CORES * own, -1), "line", axis=0, tiled=True)

    def fetch_input(layer, other):
        def of(c):
            at = rep * CORES + c
            parts = [
                lax.dynamic_slice_in_dim(input_weight[layer], part * width + at * own, own, 1)
                for part in range(3)]
            parts.append(jnp.zeros((own, start_ff - 3 * own), BF16))
            return jnp.concatenate(parts, axis=1)

        return fetch_columns(of, other)

    def fetch_expand(layer, other):
        def of(c):
            return lax.dynamic_slice_in_dim(
                expand_weight[layer], (rep * CORES + c) * own_ff, own_ff, 1)

        return fetch_columns(of, other)

    def fetch_rows(layer, other):
        def piece(matrix, padded):
            matrix = jnp.pad(matrix, ((0, padded - matrix.shape[0]), (0, 0)))
            return lax.dynamic_slice_in_dim(
                matrix, (rep ^ line) * (padded // reps), padded // reps, 0)

        rows = jnp.concatenate(
            [piece(output_weight[layer], own_up), piece(reduce_weight[layer], own_ff_up)])
        return lax.all_gather(put_back(after(rows, other)), "line", axis=0, tiled=False)

    def unpack(fetched):
        columns, rows, expand_part = fetched
        input_part = jnp.concatenate(
            [pad_heads(columns[:, part * own : (part + 1) * own]) for part in range(3)], axis=1)
        expand_part = jnp.pad(expand_part, ((0, 0), (0, wide_ff - own_ff)))
        output_part = rows[:, : own_up // reps].reshape(own_up, width)[:own]
        output_part = jnp.pad(
            output_part.reshape(heads, head_dim, width), ((0, 0), (0, LANES - head_dim), (0, 0)))
        reduce_part = rows[:, own_up // reps :].reshape(own_ff_up, width)
        reduce_part = jnp.pad(reduce_part, ((0, wide_ff - own_ff_up), (0, 0)))
        return input_part, output_part.reshape(wide, width), expand_part, reduce_part

    def spread_columns(grad):
        return lax.psum_scatter(grad.astype(BF16), "line", scatter_dimension=0, tiled=True)

    def sides(grad):
        grad = grad.reshape(CORES, own, -1)
        kept = lax.dynamic_index_in_dim(grad, core, 0, keepdims=False)
        got = swap(lax.dynamic_index_in_dim(grad, 1 - core, 0, keepdims=False))
        return jnp.where(core == 0, jnp.stack([kept, got]), jnp.stack([got, kept]))

    def every_rep(block):
        return list(lax.all_gather(block, "rep", axis=0, tiled=False))

    def in_order(blocks):
        for bit in range(bits):
            turn = (line >> bit) & 1 == 1
            blocks = [jnp.where(turn, blocks[a ^ (1 << bit)], blocks[a]) for a in range(reps)]
        return blocks

    def join_input(parts):
        parts = [part[c].astype(F32) for part in parts for c in range(CORES)]
        return jnp.concatenate(
            [part[:, k * own : (k + 1) * own] for k in range(3) for part in parts], axis=1)

    def join_expand(parts):
        return jnp.concatenate(
            [part[c].astype(F32) for part in parts for c in range(CORES)], axis=1)

    def spread_rows(grad):
        rows = grad.shape[0]
        padded = jnp.pad(grad.astype(BF16), ((0, up(rows, 16 * reps) - rows), (0, 0)))
        return lax.psum_scatter(padded, "line", scatter_dimension=0, tiled=True)

    def join_rows(parts, rows):
        return jnp.concatenate(parts)[:rows].astype(F32)

    def both(function, *pairs_of):
        return tuple(function(*each) for each in zip(*pairs_of))

    def summed(left, right):
        return dot_first(left[0], right[0]) + dot_first(left[1], right[1])

    stored = []
    weights = []
    ahead_input = fetch_input(0, small)
    for layer in range(layers):
        gain_one, shift_one = whole(0, layer), whole(1, layer)
        again, scaled_one, inverse_one = norm_forward(stream, gain_one, shift_one)
        normed_all = gather(normed if layer == 0 else again.astype(BF16))
        if layer == 0:
            ahead = (ahead_input, fetch_rows(0, normed_all[0]), fetch_expand(0, normed_all[0]))
        weights.append(unpack(ahead))
        input_part, output_part, expand_part, reduce_part = weights[layer]
        bias = jnp.concatenate(
            [pad_heads(my_part(2, layer)), jnp.zeros((wide,), F32),
             pad_heads(my_part(3, layer))])
        projected = jnp.concatenate(
            both(lambda a: (dot(a, input_part) + bias).astype(BF16), normed_all))
        attended, attended_low, log_sum = attend(
            projected, ids_column, ids_rows, counts, pairs, heads, scale)
        if layer + 1 < layers:
            ahead = (fetch_input(layer + 1, attended_low), fetch_rows(layer + 1, attended_low),
                     fetch_expand(layer + 1, attended_low))
        halves = (attended_low[: tokens // 2], attended_low[tokens // 2 :])
        middle = (stream + scatter(halves, lambda a: dot(a, output_part))
                  + whole(4, layer))
        gain_two, shift_two = whole(5, layer), whole(6, layer)
        normed_two, scaled_two, inverse_two = norm_forward(middle, gain_two, shift_two)
        normed_two_all = gather(normed_two.astype(BF16))
        expand_bias_part = jnp.pad(mine[layer, 8 * own :], (0, wide_ff - own_ff)).astype(F32)
        if layer == max(layers - 2, 0):
            upstream = relocate(after(cotangent, normed_two_all[0]))
        hidden_pre = both(lambda a: dot(a, expand_part) + expand_bias_part, normed_two_all)
        hidden = both(lambda a: gelu_tanh(a).astype(BF16), hidden_pre)
        stream = (middle + scatter(hidden, lambda a: dot(a, reduce_part))
                  + whole(7, layer))
        stored.append(
            (gain_one, scaled_one, inverse_one, normed_all, projected, attended, halves,
             log_sum, gain_two, scaled_two, inverse_two, normed_two_all, hidden_pre, hidden))

    encoded = put_back(stream.astype(BF16)).astype(F32)
    grads = [None] * layers
    spreads = [None] * layers
    packed = [None] * layers
    here = (jnp.arange(shards) == rank).astype(F32)[:, None]
    for layer in range(layers - 1, -1, -1):
        input_part, output_part, expand_part, reduce_part = weights[layer]
        (gain_one, scaled_one, inverse_one, normed_all, projected, attended, halves,
         log_sum, gain_two, scaled_two, inverse_two, normed_two_all, hidden_pre, hidden,
         ) = stored[layer]
        upstream_low = upstream.astype(BF16)
        if layer + 1 == layers:
            upstream_low = after(upstream_low, hidden[0])
        upstream_all = gather(upstream_low)
        grad_reduce_bias = jnp.sum(upstream, axis=0)
        grad_pre = both(
            lambda u, h: dot_last(u, reduce_part) * gelu_slope(h), upstream_all, hidden_pre)
        grad_pre_low = both(lambda a: a.astype(BF16), grad_pre)
        grad_expand_bias = sum(both(lambda a: jnp.sum(a, axis=0)[:own_ff], grad_pre))
        grad_normed_two = scatter(grad_pre_low, lambda a: dot_last(a, expand_part))
        grad_reduce = summed(hidden, upstream_all)[:own_ff]
        grad_expand = summed(normed_two_all, grad_pre_low)[:, :own_ff]
        part_two, grad_gain_two, grad_shift_two = norm_backward(
            grad_normed_two, scaled_two, inverse_two, gain_two)
        grad_middle = upstream + part_two
        grad_middle_all = gather(grad_middle.astype(BF16))
        grad_output_bias = jnp.sum(grad_middle, axis=0)
        grad_attended = jnp.concatenate(
            both(lambda a: dot_last(a, output_part).astype(BF16), grad_middle_all))
        grad_projected, bias_sums = attend_back(
            projected, grad_attended, attended, ids_column, ids_rows, log_sum, counts, pairs,
            heads, scale)
        grad_projected = (grad_projected[: tokens // 2], grad_projected[tokens // 2 :])
        grad_normed = scatter(grad_projected, lambda a: dot_last(a, input_part))
        grad_output = summed(halves, grad_middle_all)
        grad_output = grad_output.reshape(heads, LANES, width)[:, :head_dim]
        grad_output = grad_output.reshape(own, width)
        grad_input = summed(normed_all, grad_projected)
        grad_input = jnp.concatenate(
            [cut_heads(grad_input[:, part * wide : (part + 1) * wide]) for part in range(3)],
            axis=1)
        part_one, grad_gain_one, grad_shift_one = norm_backward(
            grad_normed, scaled_one, inverse_one, gain_one)
        upstream = grad_middle + part_one
        mlp_spread = (spread_columns(grad_expand), spread_rows(grad_reduce))
        attention_spread = (spread_columns(grad_input), spread_rows(grad_output))
        spreads[layer] = (mlp_spread, attention_spread)
        if layer + 1 < layers:
            (late_expand, late_reduce), (late_input, late_output) = spreads[layer + 1]
            late = jnp.concatenate([late_input, late_expand], axis=1)
            parts = every_rep(sides(after(late, grad_middle_all[0])))
            late = jnp.concatenate([late_output, late_reduce])
            blocks = every_rep(relocate(after(late, grad_middle_all[0])))
            blocks = in_order(blocks)
            cut_at = late_output.shape[0]
            grads[layer + 1] = (
                join_input([part[:, :, : 3 * own] for part in parts]),
                join_rows([block[:cut_at] for block in blocks], own),
                join_expand([part[:, :, 3 * own :] for part in parts]),
                join_rows([block[cut_at:] for block in blocks], own_ff))

        def cut(vector):
            return vector.reshape(shards, -1)

        sums = jnp.concatenate(
            [cut(grad_gain_one), cut(grad_shift_one), here * cut_heads(bias_sums[0]),
             here * cut_heads(bias_sums[1]), cut(grad_output_bias), cut(grad_gain_two),
             cut(grad_shift_two), cut(grad_reduce_bias), here * grad_expand_bias], axis=1)
        packed[layer] = sums

    (last_expand, last_reduce), (last_input, last_output) = spreads[0]
    grads[0] = (
        join_input(collect(sides(last_input), 0)),
        join_rows(collect(relocate(last_output), line), own),
        join_expand(every_rep(sides(after(last_expand, grad_attended)))),
        join_rows(in_order(every_rep(relocate(after(last_reduce, grad_attended)))), own_ff))
    patch_grad = put_back(upstream.astype(BF16)).astype(F32)
    sums = jnp.stack(packed)
    for hop in [mates] + rep_hops + line_hops:
        sums = sums + lax.ppermute(sums, every, hop)
    sums = lax.dynamic_index_in_dim(sums, line * CORES + core, 1, keepdims=False)
    vectors = [sums[:, index * own : (index + 1) * own] for index in range(8)]
    vectors.append(sums[:, 8 * own :])
    stacked = [
        jnp.stack([grads[layer][member] for layer in range(layers)]) for member in range(4)]
    return (
        encoded, patch_grad, stacked[0], stacked[1], stacked[2], stacked[3],
        vectors[0], vectors[1], vectors[2], vectors[3], vectors[4], vectors[5], vectors[6],
        vectors[8], vectors[7],
    )


def solution(mesh):
    reps, shards = mesh.shape["rep"], mesh.shape["fsdp"]
    assert shards == reps * CORES and reps & (reps - 1) == 0 and HEADS % shards == 0
    own = ("line", "core")
    split = Mesh(mesh.devices.reshape(reps, reps, CORES), ("rep", "line", "core"))
    tokens = P(("rep",) + own, None)
    matrix, vector = P(None, own, None), P(None, own)
    return jax.shard_map(
        functools.partial(body, reps),
        mesh=split,
        in_specs=(tokens, tokens, P("rep", None)) + (matrix,) * 4 + (vector,) * 9,
        out_specs=(tokens, tokens) + (matrix,) * 4 + (vector,) * 9,
        check_vma=False,
    )
```
